32 devices in a mesh: chan: 16 (over z, y, x), cyl: 2 (over core).
Axes of the slice: x: 2, y: 2, z: 4, core: 2. Of those that a mesh axis runs over, the one named last changes fastest.
Arguments:
- volts: bfloat16 [1024, 4, 2, 64, 512], P('chan', 'cyl'), may hold values from -6 to 6
- gain_exponents: int32 [1024, 4], P('chan', 'cyl'), may hold values from -1 to 1
Outputs:
- intensity: float32 [4, 256, 2, 16384], P('cyl', 'chan')
The draws below stay inside these ranges and needn't reach their ends.
All inputs are finite; a program needn't handle non-finite values.
Results may differ from the reference program's by a relative error of at most 0.0042.
Values may be sent and summed in bfloat16 or wider, within the bound.
A program may use at most 256 MiB of HBM per device.

```python
import math
import jax
import jax.numpy as jnp
from jax import lax

F = 1024
CYLS = 4
FEEDS = 256
POLS = 2
UP = 16
TIME = 64
FRAMES = 2
SUMS = 2
N_CYL = 2


def touch_ends(array, rng, smallest, high):
    shape = array.shape
    place = [jax.random.randint(jax.random.fold_in(rng, axis), (), 0, shape[axis]) for axis in range(len(shape))]
    array = array.at[tuple(place)].set(smallest)
    longest = shape.index(max(shape))
    place[longest] = (place[longest] + 1) % shape[longest]
    return array.at[tuple(place)].set(high)


def steps_of(own_key, extent, shards, low, largest):
    def one(axis_at, shards_of):
        heights = jax.random.uniform(jax.random.fold_in(jax.random.fold_in(own_key, 6), axis_at), (shards_of,), jnp.float32, low / len(shards), largest / len(shards))
        return jnp.repeat(jnp.exp(heights), extent[axis_at] // shards_of).reshape((-1,) + (1,) * (len(extent) - axis_at - 1))

    gain = one(*shards[0])
    for cut in shards[1:]:
        gain = gain * one(*cut)
    return gain


def centred(rng, shape, deviation, reach, cuts=(), kind=jnp.bfloat16):
    drawn = deviation * jax.random.normal(rng, shape, jnp.float32)
    if cuts:
        drawn = drawn * steps_of(rng, shape, cuts, -0.22, 0.18)
    return jnp.clip(drawn, -reach, reach).astype(kind)


def setup_inputs(seed: int = 0) -> dict:
    key_list = jax.random.split(jax.random.key(seed), 3)
    return {
        "volts": centred(key_list[0], (F, CYLS, POLS, TIME, 2 * FEEDS), 1.0, 6.0, ((0, 16), (1, 2))),
        "gain_exponents": touch_ends(jax.random.randint(key_list[1], (F, CYLS), -1, 2), jax.random.fold_in(key_list[1], 1), -1, 1).astype(jnp.int32),
    }


def ns_table(feeds):
    index = jnp.arange(feeds, dtype=jnp.int32)
    product = index[:, None] * (index[None, :] - feeds // 2) % feeds
    theta = product.astype(jnp.float32) * (2.0 * math.pi / feeds)
    cosine = jnp.cos(theta) / math.sqrt(feeds)
    sine = jnp.sin(theta) / math.sqrt(feeds)
    upper = jnp.stack([cosine, -sine], axis=-1).reshape(feeds, 2 * feeds)
    lower = jnp.stack([sine, cosine], axis=-1).reshape(feeds, 2 * feeds)
    return jnp.concatenate([upper, lower], axis=0).astype(jnp.bfloat16)

def up_table(up):
    index = jnp.arange(up, dtype=jnp.int32)
    product = index[:, None] * index[None, :] % up
    theta = product.astype(jnp.float32) * (2.0 * math.pi / up)
    cosine = jnp.cos(theta) / math.sqrt(up)
    sine = jnp.sin(theta) / math.sqrt(up)
    first = jnp.stack([cosine, -sine], axis=1)
    second = jnp.stack([sine, cosine], axis=1)
    return jnp.stack([first, second], axis=0).astype(jnp.bfloat16)

def ew_weights(beam_index, cyl_index, cyls):
    phase = 2.0 * math.pi * cyl_index[None, :].astype(jnp.float32) * (beam_index[:, None].astype(jnp.float32) - (cyls - 1) / 2.0) / cyls
    return (jnp.cos(phase) / 2.0, -jnp.sin(phase) / 2.0)

def combine(real_part, imag_part, w_real, w_imag):
    high = lax.Precision.HIGHEST
    pr = jnp.einsum('ec,ngcpt->ngept', w_real, real_part, precision=high) - jnp.einsum('ec,ngcpt->ngept', w_imag, imag_part, precision=high)
    pi = jnp.einsum('ec,ngcpt->ngept', w_real, imag_part, precision=high) + jnp.einsum('ec,ngcpt->ngept', w_imag, real_part, precision=high)
    return jnp.stack([pr, pi], axis=1)

def reference(volts, gain_exponents):
    group = 8 if F % 8 == 0 else 1
    table = ns_table(FEEDS).astype(jnp.float32)
    upper_table = up_table(UP).astype(jnp.float32)
    per_group = CYLS // N_CYL
    beam_index = jnp.arange(CYLS, dtype=jnp.int32)

    def one_block(pieces):
        block, exps = pieces
        ns_beams = lax.dot_general(table, block.astype(jnp.float32), (((0,), (4,)), ((), ())), precision=lax.Precision.HIGHEST)
        ns_beams = ns_beams.reshape(FEEDS, 2, group, CYLS, POLS, TIME)
        beams = None
        for part in range(N_CYL):
            cyl_index = part * per_group + jnp.arange(per_group, dtype=jnp.int32)
            w_real, w_imag = ew_weights(beam_index, cyl_index, CYLS)
            lo = part * per_group
            piece = combine(ns_beams[:, 0, :, lo:lo + per_group], ns_beams[:, 1, :, lo:lo + per_group], w_real, w_imag)
            piece = piece.astype(jnp.bfloat16).astype(jnp.float32)
            beams = piece if beams is None else beams + piece
        gains = jnp.exp2(exps.astype(jnp.float32))
        coded = (beams * gains[None, None, :, :, None, None]).astype(jnp.bfloat16)
        blocks = TIME // UP
        shaped = coded.astype(jnp.float32).reshape(FEEDS, 2, group, CYLS, POLS, blocks, UP)
        spectra = jnp.einsum('nrgepbk,rksm->ngepbsm', shaped, upper_table, precision=lax.Precision.HIGHEST)
        power = lax.optimization_barrier(jnp.sum(spectra * spectra, axis=(3, 5)))
        power = power.reshape(FEEDS, group, CYLS, FRAMES, SUMS, UP).sum(axis=4) / (POLS * SUMS)
        return jnp.transpose(power, (2, 0, 3, 1, 4)).reshape(CYLS, FEEDS, FRAMES, group * UP)
    shaped_volts = volts.reshape(F // group, group, CYLS, POLS, TIME, 2 * FEEDS)
    shaped_exps = gain_exponents.reshape(F // group, group, CYLS)
    result = lax.map(one_block, (shaped_volts, shaped_exps))
    result = jnp.transpose(result, (1, 2, 3, 0, 4))
    return result.reshape(CYLS, FEEDS, FRAMES, F * UP)
```

```python
import functools
import math

import jax
import jax.numpy as jnp
import ml_dtypes
import numpy as np
from jax import lax
from jax.experimental import pallas as pl
from jax.experimental.pallas import tpu as pltpu
from jax.sharding import PartitionSpec as P

UP = 16
FRAMES = 2


def ns_rows(feeds):
    index = np.arange(feeds)
    theta = (index[None, :] * (index[:, None] - feeds // 2) % feeds) * (2.0 * math.pi / feeds)
    cosine = np.cos(theta) / math.sqrt(feeds)
    sine = np.sin(theta) / math.sqrt(feeds)
    table = np.concatenate(
        [np.concatenate([cosine, sine], axis=1), np.concatenate([-sine, cosine], axis=1)], axis=0
    )
    return table.astype(ml_dtypes.bfloat16)


def fine_rows(cyls, n_cyl, up):
    index = np.arange(up)
    theta = (index[:, None] * index[None, :] % up) * (2.0 * math.pi / up)
    rounded = lambda x: (x / math.sqrt(up)).astype(ml_dtypes.bfloat16).astype(np.float64)
    fine = rounded(np.cos(theta)) - 1j * rounded(np.sin(theta))
    cyl = np.arange(cyls)
    phase = 2.0 * math.pi * cyl[None, :] * (cyl[:, None] - (cyls - 1) / 2.0) / cyls
    weight = np.exp(-1j * phase) / 2.0
    both = np.einsum("ec,km->emck", weight, fine)
    parts = np.stack(
        [np.stack([both.real, -both.imag], axis=3), np.stack([both.imag, both.real], axis=3)], axis=0
    )
    per = cyls // n_cyl
    tables = []
    for rank in range(n_cyl):
        order = [((rank - d) % n_cyl) * per + c for d in range(n_cyl) for c in range(per)]
        tables.append(parts[:, :, :, order].reshape(2 * cyls * up, cyls * 2 * up))
    return np.stack(tables).astype(ml_dtypes.bfloat16)


def beam_kernel(cyls, rank_ref, *refs):
    *volt_refs, fine_ref, ns_ref, gain_ref, out_ref, mid_ref = refs
    group, per, pols, times, inputs = volt_refs[0].shape
    feeds = inputs // 2
    blocks = times // UP
    sums = blocks // FRAMES
    fine = fine_ref[0]

    def one_chan(ch, carry):
        for p in range(pols):
            for j in range(blocks):
                rows = jnp.concatenate(
                    [
                        ref[ch, c, p, j * UP : (j + 1) * UP, r * feeds : (r + 1) * feeds]
                        for ref in volt_refs
                        for c in range(per)
                        for r in range(2)
                    ],
                    axis=0,
                )
                got = jnp.dot(fine, rows, preferred_element_type=jnp.float32).astype(jnp.bfloat16)
                for s in range(2):
                    for e in range(cyls):
                        at = (s * cyls + e) * UP
                        mid_ref[p * blocks + j, e, ch, :, s * feeds : (s + 1) * feeds] = got[at : at + UP]
        return carry

    lax.fori_loop(0, group, one_chan, 0)
    wide = group * UP
    pair = 2 if cyls % 2 == 0 else 1
    ns = ns_ref[...]
    for q in range(FRAMES):
        for e in range(0, cyls, pair):
            total = None
            for p in range(pols):
                for j in range(q * sums, (q + 1) * sums):
                    block = mid_ref[p * blocks + j, e : e + pair].reshape(pair * wide, inputs)
                    spectra = lax.dot_general(
                        ns, block, (((1,), (1,)), ((), ())), preferred_element_type=jnp.float32
                    )
                    squared = spectra * spectra
                    power = squared[:feeds] + squared[feeds:]
                    total = power if total is None else total + power
            for i in range(pair):
                scaled = total[:, i * wide : (i + 1) * wide] * gain_ref[0, e + i : e + i + 1, :]
                out_ref[0, e + i, q] = scaled.astype(jnp.bfloat16)


def local(n_chan, n_cyl, volts, gain_exponents):
    chans, per, pols, times, inputs = volts.shape
    feeds = inputs // 2
    cyls = per * n_cyl
    own = chans // n_cyl
    group = math.gcd(8, own)
    steps = own // group
    wide = group * UP
    blocks = times // UP
    rank = lax.axis_index("cyl")
    pieces = [volts]
    gains = [lax.dynamic_slice_in_dim(gain_exponents, rank * own, own, 0)]
    for d in range(1, n_cyl):
        ring = [(k, (k + d) % n_cyl) for k in range(n_cyl)]
        to = (rank + d) % n_cyl
        pieces.append(lax.ppermute(lax.dynamic_slice_in_dim(volts, to * own, own, 0), "cyl", ring))
        gains.append(
            lax.ppermute(lax.dynamic_slice_in_dim(gain_exponents, to * own, own, 0), "cyl", ring)
        )
    stacked = jnp.stack(gains)
    order = (rank - jnp.arange(n_cyl, dtype=jnp.int32)) % n_cyl
    exps = jnp.take(stacked, order, axis=0)
    exps = jnp.transpose(exps, (0, 2, 1)).reshape(cyls, steps, group)
    scale = jnp.exp2(2.0 * exps.astype(jnp.float32)) / (pols * (blocks // FRAMES))
    scale = jnp.transpose(jnp.repeat(scale, UP, axis=2), (1, 0, 2))

    volt_block = (group, per, pols, times, inputs)
    in_specs = [pl.BlockSpec(volt_block, lambda g, r: (r[0] * steps + g, 0, 0, 0, 0))]
    in_specs += [pl.BlockSpec(volt_block, lambda g, r: (g, 0, 0, 0, 0))] * (n_cyl - 1)
    fine = jnp.asarray(fine_rows(cyls, n_cyl, UP))
    ns = jnp.asarray(ns_rows(feeds))
    in_specs += [
        pl.BlockSpec((1,) + fine.shape[1:], lambda g, r: (r[0], 0, 0)),
        pl.BlockSpec(ns.shape, lambda g, r: (0, 0)),
        pl.BlockSpec((1, cyls, wide), lambda g, r: (g, 0, 0)),
    ]
    power = pl.pallas_call(
        functools.partial(beam_kernel, cyls),
        out_shape=jax.ShapeDtypeStruct((steps, cyls, FRAMES, feeds, wide), jnp.bfloat16),
        grid_spec=pltpu.PrefetchScalarGridSpec(
            num_scalar_prefetch=1,
            grid=(steps,),
            in_specs=in_specs,
            out_specs=pl.BlockSpec((1, cyls, FRAMES, feeds, wide), lambda g, r: (g, 0, 0, 0, 0)),
            scratch_shapes=[pltpu.VMEM((pols * blocks, cyls, group, UP, inputs), jnp.bfloat16)],
        ),
        compiler_params=pltpu.CompilerParams(dimension_semantics=("arbitrary",)),
        name="beams",
    )(jnp.reshape(rank, (1,)).astype(jnp.int32), *pieces, fine, ns, scale)

    near = feeds // n_chan
    power = power.reshape(steps, n_cyl, per, FRAMES, n_chan, near, wide)
    power = jnp.transpose(power, (4, 1, 2, 3, 0, 5, 6))
    power = power.reshape(n_chan * n_cyl, per, FRAMES, steps, near, wide)
    power = lax.all_to_all(power, ("chan", "cyl"), split_axis=0, concat_axis=0, tiled=True)
    power = jnp.transpose(power, (1, 4, 2, 0, 3, 5))
    return power.reshape(per, near, FRAMES, -1).astype(jnp.float32)


def solution(mesh):
    return jax.shard_map(
        functools.partial(local, mesh.shape["chan"], mesh.shape["cyl"]),
        mesh=mesh,
        in_specs=(P("chan", "cyl", None, None, None), P("chan", "cyl")),
        out_specs=P("cyl", "chan", None, None),
        check_vma=False,
    )
```

```python
import functools
import math

import jax
import jax.numpy as jnp
import ml_dtypes
import numpy as np
from jax import lax
from jax.experimental import pallas as pl
from jax.experimental.pallas import tpu as pltpu
from jax.sharding import PartitionSpec as P

UP = 16
FRAMES = 2


def ns_rows(feeds):
    index = np.arange(feeds)
    theta = (index[None, :] * (index[:, None] - feeds // 2) % feeds) * (2.0 * math.pi / feeds)
    cosine = np.cos(theta) / math.sqrt(feeds)
    sine = np.sin(theta) / math.sqrt(feeds)
    table = np.concatenate(
        [np.concatenate([cosine, sine], axis=1), np.concatenate([-sine, cosine], axis=1)], axis=0
    )
    return table.astype(ml_dtypes.bfloat16)


def fine_rows(cyls, n_cyl, up):
    index = np.arange(up)
    theta = (index[:, None] * index[None, :] % up) * (2.0 * math.pi / up)
    rounded = lambda x: (x / math.sqrt(up)).astype(ml_dtypes.bfloat16).astype(np.float64)
    fine = rounded(np.cos(theta)) - 1j * rounded(np.sin(theta))
    cyl = np.arange(cyls)
    phase = 2.0 * math.pi * cyl[None, :] * (cyl[:, None] - (cyls - 1) / 2.0) / cyls
    weight = np.exp(-1j * phase) / 2.0
    both = np.einsum("ec,km->emck", weight, fine)
    parts = np.stack(
        [np.stack([both.real, -both.imag], axis=3), np.stack([both.imag, both.real], axis=3)], axis=0
    )
    per = cyls // n_cyl
    tables = []
    for rank in range(n_cyl):
        order = [((rank - d) % n_cyl) * per + c for d in range(n_cyl) for c in range(per)]
        tables.append(parts[:, :, :, order].reshape(2 * cyls * up, cyls * 2 * up))
    return np.stack(tables).astype(ml_dtypes.bfloat16)


def beam_kernel(
    cyls, n_cyl, volts_ref, fine_ref, ns_ref, gain_ref, out_ref,
    mid_ref, held_ref, own_sem, send_sem, recv_sem,
):
    step = pl.program_id(0)
    steps = pl.num_programs(0)
    _, _, group, per, pols, times, inputs = held_ref.shape
    feeds = inputs // 2
    blocks = times // UP
    sums = blocks // FRAMES
    rank = lax.axis_index("cyl")

    def own_copy(g):
        rows = pl.ds((rank * steps + g) * group, group)
        return pltpu.make_async_copy(volts_ref.at[rows], held_ref.at[0, g], own_sem.at[g])

    def far_copy(d, g):
        to = lax.rem(rank + d, n_cyl)
        rows = pl.ds((to * steps + g) * group, group)
        return pltpu.make_async_remote_copy(
            src_ref=volts_ref.at[rows],
            dst_ref=held_ref.at[d, g],
            send_sem=send_sem.at[d, g],
            recv_sem=recv_sem.at[d, g],
            device_id={"cyl": to},
            device_id_type=pl.DeviceIdType.MESH,
        )

    @pl.when(step == 0)
    def _():
        own_copy(0).start()
        barrier = pltpu.get_barrier_semaphore()
        for d in range(1, n_cyl):
            pl.semaphore_signal(
                barrier, inc=1, device_id={"cyl": lax.rem(rank + d, n_cyl)},
                device_id_type=pl.DeviceIdType.MESH,
            )
        pl.semaphore_wait(barrier, n_cyl - 1)

        def start(g, carry):
            for d in range(1, n_cyl):
                far_copy(d, g).start()

            @pl.when(g > 0)
            def _():
                own_copy(g).start()

            return carry

        lax.fori_loop(0, steps, start, 0)

    own_copy(step).wait()
    for d in range(1, n_cyl):
        far_copy(d, step).wait()
    volt_refs = [held_ref.at[d, step] for d in range(n_cyl)]
    fine = fine_ref[rank]

    def one_chan(ch, carry):
        for p in range(pols):
            for j in range(blocks):
                rows = jnp.concatenate(
                    [
                        ref[ch, c, p, j * UP : (j + 1) * UP, r * feeds : (r + 1) * feeds]
                        for ref in volt_refs
                        for c in range(per)
                        for r in range(2)
                    ],
                    axis=0,
                )
                got = jnp.dot(fine, rows, preferred_element_type=jnp.float32).astype(jnp.bfloat16)
                for s in range(2):
                    for e in range(cyls):
                        at = (s * cyls + e) * UP
                        mid_ref[p * blocks + j, e, ch, :, s * feeds : (s + 1) * feeds] = got[at : at + UP]
        return carry

    lax.fori_loop(0, group, one_chan, 0)
    wide = group * UP
    pair = 2 if cyls % 2 == 0 else 1
    ns = ns_ref[...]
    for q in range(FRAMES):
        for e in range(0, cyls, pair):
            total = None
            for p in range(pols):
                for j in range(q * sums, (q + 1) * sums):
                    block = mid_ref[p * blocks + j, e : e + pair].reshape(pair * wide, inputs)
                    spectra = lax.dot_general(
                        ns, block, (((1,), (1,)), ((), ())), preferred_element_type=jnp.float32
                    )
                    squared = spectra * spectra
                    power = squared[:feeds] + squared[feeds:]
                    total = power if total is None else total + power
            for i in range(pair):
                scaled = total[:, i * wide : (i + 1) * wide] * gain_ref[0, e + i : e + i + 1, :]
                out_ref[0, e + i, q] = scaled.astype(jnp.bfloat16)


def spread_kernel(in_ref, out_ref):
    sources, _, frames, steps, near, wide = in_ref.shape

    def one(source, carry):
        at = pl.multiple_of(source * (steps * wide), 128)
        for g in range(steps):
            rows = [in_ref[source, 0, q, g].astype(jnp.float32) for q in range(frames)]
            out_ref[0, :, :, pl.ds(at + g * wide, wide)] = jnp.stack(rows, axis=1)
        return carry

    lax.fori_loop(0, sources, one, 0)


def spread(power):
    sources, per, frames, steps, near, wide = power.shape
    lanes = sources * steps * wide
    return pl.pallas_call(
        spread_kernel,
        out_shape=jax.ShapeDtypeStruct((per, near, frames, lanes), jnp.float32),
        grid=(per,),
        in_specs=[pl.BlockSpec((sources, 1, frames, steps, near, wide), lambda e: (0, e, 0, 0, 0, 0))],
        out_specs=pl.BlockSpec((1, near, frames, lanes), lambda e: (e, 0, 0, 0)),
        compiler_params=pltpu.CompilerParams(dimension_semantics=("arbitrary",)),
        name="spread",
    )(power)


def local(n_chan, n_cyl, volts, gain_exponents):
    chans, per, pols, times, inputs = volts.shape
    feeds = inputs // 2
    cyls = per * n_cyl
    own = chans // n_cyl
    group = math.gcd(8, own)
    steps = own // group
    wide = group * UP
    blocks = times // UP
    rank = lax.axis_index("cyl")
    gains = [lax.dynamic_slice_in_dim(gain_exponents, rank * own, own, 0)]
    for d in range(1, n_cyl):
        ring = [(k, (k + d) % n_cyl) for k in range(n_cyl)]
        to = (rank + d) % n_cyl
        gains.append(
            lax.ppermute(lax.dynamic_slice_in_dim(gain_exponents, to * own, own, 0), "cyl", ring)
        )
    stacked = jnp.stack(gains)
    order = (rank - jnp.arange(n_cyl, dtype=jnp.int32)) % n_cyl
    exps = jnp.take(stacked, order, axis=0)
    exps = jnp.transpose(exps, (0, 2, 1)).reshape(cyls, steps, group)
    scale = jnp.exp2(2.0 * exps.astype(jnp.float32)) / (pols * (blocks // FRAMES))
    scale = jnp.transpose(jnp.repeat(scale, UP, axis=2), (1, 0, 2))

    fine = jnp.asarray(fine_rows(cyls, n_cyl, UP))
    ns = jnp.asarray(ns_rows(feeds))
    power = pl.pallas_call(
        functools.partial(beam_kernel, cyls, n_cyl),
        out_shape=jax.ShapeDtypeStruct((steps, cyls, FRAMES, feeds, wide), jnp.bfloat16),
        grid=(steps,),
        in_specs=[
            pl.BlockSpec(memory_space=pl.ANY),
            pl.BlockSpec(fine.shape, lambda g: (0, 0, 0)),
            pl.BlockSpec(ns.shape, lambda g: (0, 0)),
            pl.BlockSpec((1, cyls, wide), lambda g: (g, 0, 0)),
        ],
        out_specs=pl.BlockSpec((1, cyls, FRAMES, feeds, wide), lambda g: (g, 0, 0, 0, 0)),
        scratch_shapes=[
            pltpu.VMEM((pols * blocks, cyls, group, UP, inputs), jnp.bfloat16),
            pltpu.VMEM((n_cyl, steps, group, per, pols, times, inputs), jnp.bfloat16),
            pltpu.SemaphoreType.DMA((steps,)),
            pltpu.SemaphoreType.DMA((n_cyl, steps)),
            pltpu.SemaphoreType.DMA((n_cyl, steps)),
        ],
        compiler_params=pltpu.CompilerParams(
            dimension_semantics=("arbitrary",), collective_id=0, has_side_effects=True
        ),
        name="beams",
    )(volts, fine, ns, scale)

    near = feeds // n_chan
    power = power.reshape(steps, n_cyl, per, FRAMES, n_chan, near, wide)
    power = jnp.transpose(power, (4, 1, 2, 3, 0, 5, 6))
    power = power.reshape(n_chan * n_cyl, per, FRAMES, steps, near, wide)
    power = lax.all_to_all(power, ("chan", "cyl"), split_axis=0, concat_axis=0, tiled=True)
    if (steps * wide) % 128 == 0:
        return spread(power)
    power = jnp.transpose(power, (1, 4, 2, 0, 3, 5))
    return power.reshape(per, near, FRAMES, -1).astype(jnp.float32)


def solution(mesh):
    return jax.shard_map(
        functools.partial(local, mesh.shape["chan"], mesh.shape["cyl"]),
        mesh=mesh,
        in_specs=(P("chan", "cyl", None, None, None), P("chan", "cyl")),
        out_specs=P("cyl", "chan", None, None),
        check_vma=False,
    )
```
